32 devices in a mesh: tm: 4 (over y, x), space: 8 (over z, core).
Axes of the slice: x: 2, y: 2, z: 4, core: 2. Of those that a mesh axis runs over, the one named last changes fastest.
Arguments:
- vectors: bfloat16 [8, 2, 3, 4096, 384], P('tm', None, None, 'space'), may hold values from -6 to 6
- perambulators: bfloat16 [32, 2, 384, 384], P(('tm', 'space')), may hold values from -0.0014648438 to 0.0014648438
- item_block: int32 [32, 32], P(('tm', 'space')), may hold values from 0 to 3
- item_owner: int32 [32, 32], P(('tm', 'space')), may hold values from 0 to 31, as said below
- momenta: int32 [2, 3], replicated, may hold values from -2 to 2, as said below
Outputs:
- contracted: bfloat16 [32, 32, 2, 48, 768], P(('tm', 'space'))
The draws below stay inside these ranges and needn't reach their ends.
Inputs may be any that keep to these rules, and one draw needn't show every extreme that they name: `item_owner`: in every device's list no owner appears more than 2 times, and some owners appear exactly 2 times in the lists of all devices. `momenta`: the first component of every momentum is nonzero.
All inputs are finite; a program needn't handle non-finite values.
Results may differ from the reference program's by a relative error of at most 0.0057.
Values may be sent and summed in bfloat16 or wider, within the bound.
No kernel may reach another device: no remote copies, remote signals or barrier semaphores. Data moves between devices by JAX's collectives and lax.ppermute only.
A program may use at most 128 MiB of HBM per device.

```python
import math
import jax
import jax.numpy as jnp
from jax import lax

N_EV = 384
LX = 64
NMOM = 2
CAP = 2
TS_DEV = 2
RB = 48
BLK = 4
T_SLAB = 8
SITES = 4096
ITEMS = 32
N_TM = 4
N_SPACE = 8
DEVICES = 32


def draw_item_owner(key, part):
    shuffle_key = jax.random.fold_in(key, 101)
    noise_key = jax.random.fold_in(key, 102)
    order_key = jax.random.fold_in(key, 103)
    heavy_count = max(1, DEVICES // 16)
    owner_order = jax.random.permutation(shuffle_key, DEVICES)
    owner_rank = jnp.zeros((DEVICES,), jnp.int32).at[owner_order].set(jnp.arange(DEVICES, dtype=jnp.int32))
    position_list = jnp.arange(DEVICES * CAP, dtype=jnp.int32)
    position_owner = position_list // CAP
    heavy_slot = owner_rank[position_owner] < heavy_count
    noise_draw = jax.random.randint(noise_key, (DEVICES, DEVICES * CAP), 0, 1 << 20)
    scores = jnp.where(heavy_slot[None, :], (1 << 29) + position_list[None, :], noise_draw * (DEVICES * CAP) + position_list[None, :])
    top_scores, picked = lax.top_k(scores, ITEMS)
    mixing = jax.random.randint(order_key, (DEVICES, ITEMS), 0, 1 << 20) * ITEMS + jnp.arange(ITEMS, dtype=jnp.int32)[None, :]
    arrangement = jnp.argsort(mixing, axis=1)
    picked = jnp.take_along_axis(picked, arrangement, axis=1)
    return position_owner[picked].astype(jnp.int32)


def draw_momenta(key, part):
    magnitude = jax.random.randint(jax.random.fold_in(key, 201), (NMOM,), 1, 3)
    direction_sign = jax.random.randint(jax.random.fold_in(key, 202), (NMOM,), 0, 2) * 2 - 1
    remaining = jax.random.randint(jax.random.fold_in(key, 203), (NMOM, 2), -2, 3)
    return jnp.concatenate([(magnitude * direction_sign)[:, None], remaining], axis=1).astype(jnp.int32)


def set_ends(array, rng, low, largest):
    longest = array.shape.index(max(array.shape))
    spots = []
    for shift in (0, 1):
        where = [jax.random.randint(jax.random.fold_in(rng, axis), (), 0, length) for axis, length in enumerate(array.shape)]
        where[longest] = (where[longest] + shift) % array.shape[longest]
        spots.append(tuple(where))
    return array.at[spots[0]].set(low).at[spots[1]].set(largest)


def block_levels(stream_key, extent, cuts, smallest, top_value):
    def one(dim, parts):
        steps = jax.random.uniform(jax.random.fold_in(jax.random.fold_in(stream_key, 6), dim), (parts,), jnp.float32, smallest / len(cuts), top_value / len(cuts))
        return jnp.repeat(jnp.exp(steps), extent[dim] // parts).reshape((-1,) + (1,) * (len(extent) - dim - 1))

    loudness = one(*cuts[0])
    for cut in cuts[1:]:
        loudness = loudness * one(*cut)
    return loudness


def scatter_about(rng, shape, deviation, reach, pieces=(), held_as=jnp.bfloat16):
    drawn = jax.random.normal(rng, shape, jnp.float32) * deviation
    if len(pieces) > 0:
        drawn = block_levels(rng, shape, pieces, -0.22, 0.18) * drawn
    return jnp.clip(drawn, min=-reach, max=reach).astype(held_as)


def setup_inputs(seed: int = 0) -> dict:
    key_of = jax.random.split(jax.random.key(seed), 6)
    return {
        "vectors": scatter_about(key_of[0], (T_SLAB, 2, 3, SITES, N_EV), 1.0, 6.0, ((0, 4), (3, 8))),
        "perambulators": scatter_about(key_of[1], (DEVICES, 2, N_EV, N_EV), (12 * N_EV * SITES) ** -0.5, 0.0014648438, ((0, 32),)),
        "item_block": set_ends(jax.random.randint(key_of[2], (DEVICES, ITEMS), 0, BLK), jax.random.fold_in(key_of[2], 1), 0, BLK - 1).astype(jnp.int32),
        "item_owner": draw_item_owner(jax.random.fold_in(key_of[5], 71), 0),
        "momenta": draw_momenta(jax.random.fold_in(key_of[5], 71), 0),
    }


def site_phase(momenta, first_site, site_count):
    site_index = first_site + jnp.arange(site_count, dtype=jnp.int32)
    coord_x = site_index % LX
    coord_y = (site_index // LX) % LX
    coord_z = site_index // (LX * LX)
    phase_turns = (momenta[:, 0:1] * coord_x[None, :] + momenta[:, 1:2] * coord_y[None, :] + momenta[:, 2:3] * coord_z[None, :]) % LX
    phase_angle = phase_turns.astype(jnp.float32) * (2.0 * math.pi / LX)
    return jnp.cos(phase_angle), jnp.sin(phase_angle)


def twisted_right(vectors, cosines, sines):
    real_part = vectors[:, 0].astype(jnp.float32)[:, None]
    imag_part = vectors[:, 1].astype(jnp.float32)[:, None]
    cosine = cosines[None, :, None, :, None]
    sine_term = sines[None, :, None, :, None]
    twisted_real = (cosine * real_part + sine_term * imag_part).astype(jnp.bfloat16)
    twisted_imag = (cosine * imag_part - sine_term * real_part).astype(jnp.bfloat16)
    upper_half = jnp.stack([twisted_real, twisted_imag], axis=2)
    lower_half = jnp.stack([twisted_imag, -twisted_real], axis=2)
    shape_lead = upper_half.shape
    inner_rows = shape_lead[2] * shape_lead[3] * shape_lead[4]
    return jnp.concatenate([upper_half.reshape(shape_lead[0], shape_lead[1], inner_rows, shape_lead[5]), lower_half.reshape(shape_lead[0], shape_lead[1], inner_rows, shape_lead[5])], axis=-1)


def slot_table(block_ids, owners, devices, pad_block):
    item_count = owners.shape[0]
    position_list = jnp.arange(item_count, dtype=jnp.int32)
    earlier = (owners[None, :] == owners[:, None]) & (position_list[None, :] < position_list[:, None])
    slot_rank = jnp.sum(earlier.astype(jnp.int32), axis=1)
    target = owners * CAP + slot_rank
    return jnp.full((devices * CAP,), pad_block, jnp.int32).at[target].set(block_ids.astype(jnp.int32))


def complex_kernel(pair):
    top_rows = jnp.concatenate([pair[0], pair[1]], axis=1)
    bottom_rows = jnp.concatenate([-pair[1], pair[0]], axis=1)
    return jnp.concatenate([top_rows, bottom_rows], axis=0)


def reference(vectors, perambulators, item_block, item_owner, momenta):
    cosines, sines = site_phase(momenta, 0, SITES)
    elementals = []
    for slab_index in range(T_SLAB):
        right_side = twisted_right(vectors[slab_index:slab_index + 1], cosines, sines)[0]
        left_side = vectors[slab_index].reshape(-1, N_EV)
        per_mom = [jnp.dot(left_side.T, right_side[mom_index], preferred_element_type=jnp.float32) for mom_index in range(NMOM)]
        elementals.append(jnp.stack(per_mom))
    elemental = jnp.stack(elementals).astype(jnp.bfloat16)
    blocks = elemental.reshape(N_TM, TS_DEV, NMOM, N_SPACE, RB, 2 * N_EV).transpose(0, 3, 1, 2, 4, 5).reshape(DEVICES, BLK, RB, 2 * N_EV)
    blocks = jnp.concatenate([blocks, jnp.zeros((DEVICES, 1, RB, 2 * N_EV), jnp.bfloat16)], axis=1)
    tables = jax.vmap(lambda block_ids, owners: slot_table(block_ids, owners, DEVICES, BLK))(item_block, item_owner)
    senders = jnp.arange(DEVICES, dtype=jnp.int32)

    def per_owner(owner_index):
        block_slots = lax.dynamic_slice_in_dim(tables, (owner_index * CAP).astype(jnp.int32), CAP, 1)
        chosen = blocks[senders[:, None], block_slots]
        kernel = complex_kernel(lax.dynamic_index_in_dim(perambulators, owner_index, 0, keepdims=False))
        product = jnp.dot(chosen.reshape(-1, 2 * N_EV), kernel, preferred_element_type=jnp.float32)
        return product.astype(jnp.bfloat16).reshape(DEVICES, CAP, RB, 2 * N_EV)

    return lax.map(per_owner, senders)
```

```python
import math

import jax
import jax.numpy as jnp
from jax import lax
from jax.experimental import pallas as pl
from jax.experimental.pallas import tpu as pltpu
from jax.sharding import PartitionSpec as P

LX = 64
CAP = 2


def site_phase(momenta, first_site, site_count):
    site_index = first_site + lax.broadcasted_iota(jnp.int32, (site_count, 1), 0)
    coord_x = site_index % LX
    coord_y = site_index // LX % LX
    coord_z = site_index // (LX * LX)
    turns = (
        coord_x * momenta[:, 0][None, :]
        + coord_y * momenta[:, 1][None, :]
        + coord_z * momenta[:, 2][None, :]
    ) % LX
    angle = turns.astype(jnp.float32) * (2.0 * math.pi / LX)
    return jnp.stack([jnp.cos(angle), jnp.sin(angle)], axis=-1).reshape(site_count, -1)


def partial_kernel(phase_ref, vec_ref, out_ref, rhs, lhs):
    color = pl.program_id(0)
    sites, width = vec_ref.shape[-2:]
    real = vec_ref[0, 0, 0]
    imag = vec_ref[0, 1, 0]
    lhs[:, :sites] = real.T
    lhs[:, sites:] = imag.T
    real = real.astype(jnp.float32)
    imag = imag.astype(jnp.float32)
    for p in range(out_ref.shape[0]):
        cosine = phase_ref[:, 2 * p : 2 * p + 1]
        sine = phase_ref[:, 2 * p + 1 : 2 * p + 2]
        twisted_real = (cosine * real + sine * imag).astype(jnp.bfloat16)
        twisted_imag = (cosine * imag - sine * real).astype(jnp.bfloat16)
        rhs[p, :sites, :width] = twisted_real
        rhs[p, sites:, :width] = twisted_imag
        rhs[p, :sites, width:] = twisted_imag
        rhs[p, sites:, width:] = -twisted_real
    for p in range(out_ref.shape[0]):
        term = jnp.dot(lhs[...], rhs[p], preferred_element_type=jnp.float32)

        @pl.when(color == 0)
        def _():
            out_ref[p] = term

        @pl.when(color > 0)
        def _():
            out_ref[p] += term


def partial_elemental(vectors, phase, slab):
    _, _, colors, sites, width = vectors.shape
    momentum_count = phase.shape[1] // 2
    return pl.pallas_call(
        partial_kernel,
        grid=(colors,),
        in_specs=[
            pl.BlockSpec(phase.shape, lambda c: (0, 0)),
            pl.BlockSpec((1, 2, 1, sites, width), lambda c: (slab, 0, c, 0, 0)),
        ],
        out_specs=pl.BlockSpec((momentum_count, width, 2 * width), lambda c: (0, 0, 0)),
        out_shape=jax.ShapeDtypeStruct((momentum_count, width, 2 * width), jnp.float32),
        scratch_shapes=[
            pltpu.VMEM((momentum_count, 2 * sites, 2 * width), jnp.bfloat16),
            pltpu.VMEM((width, 2 * sites), jnp.bfloat16),
        ],
        cost_estimate=pl.CostEstimate(
            flops=8 * momentum_count * colors * sites * width * width,
            bytes_accessed=4 * colors * sites * width + 8 * momentum_count * width * width,
            transcendentals=0,
        ),
    )(phase, vectors)


def flip(value, axis, mask):
    count = lax.axis_size(axis)
    return lax.ppermute(value, axis, [(i, i ^ mask) for i in range(count)])


def reduce_rows(partial, space_bits):
    momentum_count, width, full_width = partial.shape
    me = lax.axis_index("space")
    held = partial.reshape(momentum_count, 1 << space_bits, -1, full_width)
    for bit in range(space_bits):
        held = held.reshape(momentum_count, -1, 2, *held.shape[-2:])
        mine = (me >> bit) & 1
        keep = lax.dynamic_index_in_dim(held, mine, 2, keepdims=False)
        send = lax.dynamic_index_in_dim(held, 1 - mine, 2, keepdims=False)
        got = flip(send.astype(jnp.bfloat16), "space", 1 << bit)
        held = keep + got.astype(jnp.float32)
    return held[:, 0].astype(jnp.bfloat16)


def doubled(value, axis, masks):
    order = [0]
    for mask in masks:
        value = jnp.concatenate([value, flip(value, axis, mask)], axis=0)
        order = order + [o ^ mask for o in order]
    return value, order


def slot_table(block_ids, owners, devices, pad_block):
    item_count = owners.shape[0]
    position_list = jnp.arange(item_count, dtype=jnp.int32)
    earlier = (owners[None, :] == owners[:, None]) & (
        position_list[None, :] < position_list[:, None]
    )
    slot_rank = jnp.sum(earlier.astype(jnp.int32), axis=1)
    target = owners * CAP + slot_rank
    hit = target[:, None] == jnp.arange(devices * CAP, dtype=jnp.int32)[None, :]
    return pad_block + jnp.sum(
        jnp.where(hit, (block_ids - pad_block)[:, None], 0), axis=0
    )


def contract(meta, kernel, sources, output, out_shape, space_bits):
    slab_count = len(sources[0][1])
    momentum_count, rows, full_width = sources[0][1][0].shape[1:]
    padded = -(-rows // 16) * 16
    listing = [
        (index, position, tm_mask, space_mask)
        for index, (masks, _) in enumerate(sources)
        for position, (tm_mask, space_mask) in enumerate(masks)
    ]
    sender_count = len(listing)

    def body(meta_ref, kernel_ref, *refs):
        arrays = refs[: len(sources) * slab_count]
        out_ref, lhs, staged, sem = refs[-4:]
        my_tm = meta_ref[0]
        my_space = meta_ref[1]
        for n, (index, position, tm_mask, space_mask) in enumerate(listing):
            relative = (tm_mask << space_bits) | space_mask
            for s in range(CAP):
                block = meta_ref[2 + relative * CAP + s]
                p = block % momentum_count
                u = block // momentum_count
                value = jnp.zeros((rows, full_width), jnp.bfloat16)
                for slab in range(slab_count):
                    taken = arrays[index * slab_count + slab][position, p]
                    value = jnp.where(u == slab, taken, value)
                lhs[pl.ds((n * CAP + s) * padded, rows), :] = value
        half = sender_count // 2 if sender_count % 2 == 0 else sender_count
        copies = []
        for first in range(0, sender_count, half):
            span = half * CAP * padded
            result = jnp.dot(
                lhs[pl.ds(first * CAP * padded, span), :],
                kernel_ref[...],
                preferred_element_type=jnp.float32,
            ).astype(jnp.bfloat16)
            for n in range(first, first + half):
                for s in range(CAP):
                    at = ((n - first) * CAP + s) * padded
                    staged[n, s] = result[at : at + rows]
            for n in range(first, first + half):
                _, _, tm_mask, space_mask = listing[n]
                sender = ((my_tm ^ tm_mask) << space_bits) | (my_space ^ space_mask)
                copy = pltpu.make_async_copy(staged.at[n], out_ref.at[sender], sem.at[n])
                copy.start()
                copies.append(copy)
        for copy in copies:
            copy.wait()

    arrays = [a for _, per_slab in sources for a in per_slab]
    operands = [meta, kernel, *arrays]
    specs = [pl.BlockSpec(memory_space=pltpu.SMEM)] + [
        pl.BlockSpec(memory_space=pltpu.VMEM) for _ in operands[1:]
    ]
    aliases = {}
    if output is not None:
        aliases = {len(operands): 0}
        operands.append(output)
        specs.append(pl.BlockSpec(memory_space=pl.ANY))
    total = sender_count * CAP * padded
    return pl.pallas_call(
        body,
        in_specs=specs,
        out_specs=pl.BlockSpec(memory_space=pl.ANY),
        out_shape=jax.ShapeDtypeStruct(out_shape, jnp.bfloat16),
        input_output_aliases=aliases,
        scratch_shapes=[
            pltpu.VMEM((total, full_width), jnp.bfloat16),
            pltpu.VMEM((sender_count, CAP, rows, full_width), jnp.bfloat16),
            pltpu.SemaphoreType.DMA((sender_count,)),
        ],
        cost_estimate=pl.CostEstimate(
            flops=2 * total * full_width * full_width,
            bytes_accessed=4 * total * full_width,
            transcendentals=0,
        ),
    )(*operands)


def complex_kernel(pair):
    top_rows = jnp.concatenate([pair[0], pair[1]], axis=1)
    bottom_rows = jnp.concatenate([-pair[1], pair[0]], axis=1)
    return jnp.concatenate([top_rows, bottom_rows], axis=0)


def body(vectors, perambulators, item_block, item_owner, momenta):
    group_count = lax.axis_size("tm")
    space_count = lax.axis_size("space")
    tm_bits = group_count.bit_length() - 1
    space_bits = space_count.bit_length() - 1
    assert group_count == 1 << tm_bits and space_count == 1 << space_bits
    devices = group_count * space_count
    slab_count, _, _, site_count, width = vectors.shape
    momentum_count = momenta.shape[0]
    my_tm = lax.axis_index("tm")
    my_space = lax.axis_index("space")
    phase = site_phase(momenta, my_space * site_count, site_count)
    kernel = complex_kernel(perambulators[0])
    pad_block = slab_count * momentum_count

    table = slot_table(item_block[0], item_owner[0], devices, pad_block)[None]
    table, space_order = doubled(table, "space", [1 << b for b in reversed(range(space_bits))])
    table, tm_order = doubled(table, "tm", [1 << b for b in range(tm_bits)])
    me = my_tm * space_count + my_space
    mine = lax.dynamic_slice_in_dim(table, me * CAP, CAP, axis=1)
    place = {(t << space_bits) | s: i * space_count + j for i, t in enumerate(tm_order) for j, s in enumerate(space_order)}
    mine = jnp.concatenate([mine[place[r]] for r in range(devices)])
    meta = jnp.concatenate([jnp.stack([my_tm, my_space]).astype(jnp.int32), mine])

    chip_masks = [1 << b for b in reversed(range(1, space_bits))]
    per_slab = []
    for slab in range(slab_count):
        own = reduce_rows(partial_elemental(vectors, phase, slab), space_bits)
        line, order = doubled(own[None], "space", chip_masks)
        pieces = [((0, order), line)]
        if tm_bits == 2:
            cut = line.shape[0] // 2
            by_first = flip(line, "tm", 1)
            by_second = flip(line, "tm", 2)
            pieces.append(((1, order), by_first))
            pieces.append(((2, order), by_second))
            pieces.append(((3, order[:cut]), flip(by_first[:cut], "tm", 2)))
            pieces.append(((3, order[cut:]), flip(by_second[cut:], "tm", 1)))
        else:
            for bit in range(tm_bits):
                for (mask, masks), value in list(pieces):
                    pieces.append(((mask ^ (1 << bit), masks), flip(value, "tm", 1 << bit)))
        per_slab.append([(key, value, flip(value, "space", 1)) for key, value in pieces])
    out_shape = (devices, CAP, width // space_count, 2 * width)
    output = None
    for index in range(len(per_slab[0])):
        mask, order = per_slab[0][index][0]
        sources = [
            ([(mask, o) for o in order], [s[index][1] for s in per_slab]),
            ([(mask, o ^ 1) for o in order], [s[index][2] for s in per_slab]),
        ]
        output = contract(meta, kernel, sources, output, out_shape, space_bits)
    return output[None]


def solution(mesh):
    in_specs = (
        P("tm", None, None, "space", None),
        P(("tm", "space"), None, None, None),
        P(("tm", "space"), None),
        P(("tm", "space"), None),
        P(),
    )
    out_specs = P(("tm", "space"), None, None, None, None)
    return jax.shard_map(body, mesh=mesh, in_specs=in_specs, out_specs=out_specs, check_vma=False)
```

```python
import math

import jax
import jax.numpy as jnp
from jax import lax
from jax.experimental import pallas as pl
from jax.experimental.pallas import tpu as pltpu
from jax.sharding import PartitionSpec as P

LX = 64
CAP = 2


def site_phase(momenta, first_site, site_count):
    site_index = first_site + lax.broadcasted_iota(jnp.int32, (site_count, 1), 0)
    coord_x = site_index % LX
    coord_y = site_index // LX % LX
    coord_z = site_index // (LX * LX)
    turns = (
        coord_x * momenta[:, 0][None, :]
        + coord_y * momenta[:, 1][None, :]
        + coord_z * momenta[:, 2][None, :]
    ) % LX
    angle = turns.astype(jnp.float32) * (2.0 * math.pi / LX)
    return jnp.stack([jnp.cos(angle), jnp.sin(angle)], axis=-1).reshape(site_count, -1)


def partial_elemental(vectors, phase, slab, space_bits):
    _, _, colors, sites, width = vectors.shape
    momentum_count = phase.shape[1] // 2
    rows = width >> space_bits
    aligned = rows % 16 == 0
    depth = colors * sites
    half = width // 2

    def body(phase_ref, vec_ref, *refs):
        outs, (lhs, rhs) = refs[:-2], refs[-2:]
        me = lax.axis_index("space")
        for c in range(colors):
            for part in range(2):
                turned = vec_ref[slab, part, c].T
                columns = slice(part * depth + c * sites, part * depth + (c + 1) * sites)
                if aligned:
                    for block in range(1 << space_bits):
                        spot = 0
                        for bit in range(space_bits):
                            spot = spot * 2 + (((me ^ block) >> bit) & 1)
                        first = pl.multiple_of(spot * rows, rows)
                        lhs[pl.ds(first, rows), columns] = turned[block * rows : (block + 1) * rows]
                else:
                    lhs[:, columns] = turned
        for p in range(momentum_count):
            cosine = phase_ref[:, 2 * p : 2 * p + 1]
            sine = phase_ref[:, 2 * p + 1 : 2 * p + 2]
            for c in range(colors):
                real = vec_ref[slab, 0, c].astype(jnp.float32)
                imag = vec_ref[slab, 1, c].astype(jnp.float32)
                twisted_real = (cosine * real + sine * imag).astype(jnp.bfloat16)
                twisted_imag = (cosine * imag - sine * real).astype(jnp.bfloat16)
                upper = slice(c * sites, (c + 1) * sites)
                lower = slice(depth + c * sites, depth + (c + 1) * sites)
                rhs[p, upper, :width] = twisted_real
                rhs[p, lower, :width] = twisted_imag
                rhs[p, upper, width:] = twisted_imag
                rhs[p, lower, width:] = -twisted_real
        for p in range(momentum_count):
            if aligned:
                outs[1][p] = jnp.dot(
                    lhs[half:], rhs[p], preferred_element_type=jnp.float32
                ).astype(jnp.bfloat16)
                outs[0][p] = jnp.dot(lhs[:half], rhs[p], preferred_element_type=jnp.float32)
            else:
                outs[0][p] = jnp.dot(lhs[...], rhs[p], preferred_element_type=jnp.float32)

    if aligned:
        out_shape = [
            jax.ShapeDtypeStruct((momentum_count, half, 2 * width), jnp.float32),
            jax.ShapeDtypeStruct((momentum_count, half, 2 * width), jnp.bfloat16),
        ]
    else:
        out_shape = [jax.ShapeDtypeStruct((momentum_count, width, 2 * width), jnp.float32)]
    outs = pl.pallas_call(
        body,
        in_specs=[pl.BlockSpec(memory_space=pltpu.VMEM)] * 2,
        out_specs=[pl.BlockSpec(memory_space=pltpu.VMEM)] * len(out_shape),
        out_shape=out_shape,
        scratch_shapes=[
            pltpu.VMEM((width, 2 * depth), jnp.bfloat16),
            pltpu.VMEM((momentum_count, 2 * depth, 2 * width), jnp.bfloat16),
        ],
        cost_estimate=pl.CostEstimate(
            flops=8 * momentum_count * depth * width * width,
            bytes_accessed=4 * depth * width + 6 * momentum_count * width * width,
            transcendentals=0,
        ),
    )(phase, vectors)
    blocks = (momentum_count, 1 << (space_bits - 1), rows, 2 * width)
    if aligned:
        return outs[0].reshape(blocks), outs[1].reshape(blocks)
    spots = jnp.arange(1 << space_bits, dtype=jnp.int32)
    masks = sum(((spots >> (space_bits - 1 - b)) & 1) << b for b in range(space_bits))
    whole = outs[0].reshape(momentum_count, 1 << space_bits, rows, 2 * width)
    ordered = jnp.take(whole, lax.axis_index("space") ^ masks, axis=1)
    return ordered[:, : blocks[1]], ordered[:, blocks[1] :].astype(jnp.bfloat16)


def flip(value, axis, mask):
    count = lax.axis_size(axis)
    return lax.ppermute(value, axis, [(i, i ^ mask) for i in range(count)])


def reduce_rows(keep, send, space_bits):
    for bit in range(space_bits):
        if bit:
            cut = held.shape[1] // 2
            keep, send = held[:, :cut], held[:, cut:].astype(jnp.bfloat16)
        held = keep + flip(send, "space", 1 << bit).astype(jnp.float32)
    return held[:, 0].astype(jnp.bfloat16)


def slot_table(block_ids, owners, devices, pad_block):
    item_count = owners.shape[0]
    position_list = jnp.arange(item_count, dtype=jnp.int32)
    earlier = (owners[None, :] == owners[:, None]) & (
        position_list[None, :] < position_list[:, None]
    )
    slot_rank = jnp.sum(earlier.astype(jnp.int32), axis=1)
    target = owners * CAP + slot_rank
    hit = target[:, None] == jnp.arange(devices * CAP, dtype=jnp.int32)[None, :]
    return pad_block + jnp.sum(
        jnp.where(hit, (block_ids - pad_block)[:, None], 0), axis=0
    )


def contract(kernel, pieces, output, devices, rows, space_bits):
    slab_count = len(pieces[0][1])
    full_width = kernel.shape[0]
    momentum_count = pieces[0][1][-1].shape[1] // rows
    padded = -(-rows // 16) * 16
    listing = [
        (index, position, masks)
        for index, (senders, _) in enumerate(pieces)
        for position, masks in enumerate(senders)
    ]
    sender_count = len(listing)
    batch = min(sender_count, 4)
    assert sender_count % batch == 0

    def body(kernel_ref, *refs):
        arrays = refs[: len(pieces) * slab_count]
        out_ref, lhs, staged, sem = refs[-4:]
        my_tm = lax.axis_index("tm")
        my_space = lax.axis_index("space")
        lane = ((my_tm << space_bits) | my_space) * CAP
        lanes = lax.broadcasted_iota(jnp.int32, (16, full_width), 1)
        copies = []
        for first in range(0, sender_count, batch):
            for n in range(first, first + batch):
                index, position, _ = listing[n]
                per_slab = arrays[index * slab_count : (index + 1) * slab_count]
                tail = momentum_count * rows
                entries = per_slab[0][position, tail : tail + 16].astype(jnp.float32)
                for s in range(CAP):
                    listed = jnp.sum(jnp.where(lanes == lane + s, entries, 0.0), axis=1, keepdims=True)[0:1]
                    value = None
                    for block in range(slab_count * momentum_count):
                        p = block % momentum_count
                        taken = per_slab[block // momentum_count][position, p * rows : (p + 1) * rows]
                        weight = jnp.where(listed == block, 1.0, 0.0)
                        term = taken * jnp.broadcast_to(weight, taken.shape).astype(jnp.bfloat16)
                        value = term if value is None else value + term
                    lhs[pl.ds((n * CAP + s) * padded, rows), :] = value
            result = jnp.dot(
                lhs[pl.ds(first * CAP * padded, batch * CAP * padded), :],
                kernel_ref[...],
                preferred_element_type=jnp.float32,
            ).astype(jnp.bfloat16)
            for n in range(first, first + batch):
                for s in range(CAP):
                    at = ((n - first) * CAP + s) * padded
                    staged[n, s] = result[at : at + rows]
            for n in range(first, first + batch):
                tm_mask, space_mask = listing[n][2]
                sender = ((my_tm ^ tm_mask) << space_bits) | (my_space ^ space_mask)
                copy = pltpu.make_async_copy(staged.at[n], out_ref.at[sender], sem.at[n])
                copy.start()
                copies.append(copy)
        for copy in copies:
            copy.wait()

    operands = [kernel, *[a for _, per_slab in pieces for a in per_slab]]
    specs = [pl.BlockSpec(memory_space=pltpu.VMEM) for _ in operands]
    aliases = {}
    if output is not None:
        aliases = {len(operands): 0}
        operands.append(output)
        specs.append(pl.BlockSpec(memory_space=pl.ANY))
    total = sender_count * CAP * padded
    return pl.pallas_call(
        body,
        in_specs=specs,
        out_specs=pl.BlockSpec(memory_space=pl.ANY),
        out_shape=jax.ShapeDtypeStruct((devices, CAP, rows, full_width), jnp.bfloat16),
        input_output_aliases=aliases,
        scratch_shapes=[
            pltpu.VMEM((total, full_width), jnp.bfloat16),
            pltpu.VMEM((sender_count, CAP, rows, full_width), jnp.bfloat16),
            pltpu.SemaphoreType.DMA((sender_count,)),
        ],
        cost_estimate=pl.CostEstimate(
            flops=2 * total * full_width * full_width,
            bytes_accessed=4 * total * full_width,
            transcendentals=0,
        ),
    )(*operands)


def complex_kernel(pair):
    top_rows = jnp.concatenate([pair[0], pair[1]], axis=1)
    bottom_rows = jnp.concatenate([-pair[1], pair[0]], axis=1)
    return jnp.concatenate([top_rows, bottom_rows], axis=0)


def spread(unit, space_bits, tm_bits):
    line = [((0,), unit[None])]
    for bit in reversed(range(1, space_bits)):
        mask = 1 << bit
        held = line[0][1] if len(line) == 1 else jnp.concatenate([a for _, a in line], axis=0)
        order = sum((o for o, _ in line), ())
        line = [(order, held), (tuple(o ^ mask for o in order), flip(held, "space", mask))]
    found = [(0, order, held) for order, held in line]
    if tm_bits == 2 and len(line) == 2:
        first = [flip(held, "tm", 1) for _, held in line]
        second = [flip(held, "tm", 2) for _, held in line]
        far = [flip(first[0], "tm", 2), flip(second[1], "tm", 1)]
        for mask, arrays in ((1, first), (2, second), (3, far)):
            found += [(mask, order, a) for (order, _), a in zip(line, arrays)]
    else:
        for bit in range(tm_bits):
            found += [(mask ^ (1 << bit), order, flip(a, "tm", 1 << bit)) for mask, order, a in found]
    return found


def body(vectors, perambulators, item_block, item_owner, momenta):
    group_count = lax.axis_size("tm")
    space_count = lax.axis_size("space")
    tm_bits = group_count.bit_length() - 1
    space_bits = space_count.bit_length() - 1
    assert group_count == 1 << tm_bits and space_count == 1 << space_bits
    devices = group_count * space_count
    slab_count, _, _, site_count, width = vectors.shape
    momentum_count = momenta.shape[0]
    rows = width // space_count
    phase = site_phase(momenta, lax.axis_index("space") * site_count, site_count)
    kernel = complex_kernel(perambulators[0])
    table = slot_table(item_block[0], item_owner[0], devices, slab_count * momentum_count)
    assert devices * CAP <= 2 * width and slab_count * momentum_count < 256
    tail = jnp.pad(table.astype(jnp.bfloat16)[None], ((0, 15), (0, 2 * width - devices * CAP)))

    partials = [partial_elemental(vectors, phase, slab, space_bits) for slab in range(slab_count)]
    found = []
    for slab, (keep, send) in enumerate(partials):
        unit = reduce_rows(keep, send, space_bits).reshape(momentum_count * rows, 2 * width)
        if slab == 0:
            unit = jnp.concatenate([unit, tail], axis=0)
        pieces = spread(unit, space_bits, tm_bits)
        found.append([(mask, order, a, flip(a, "space", 1)) for mask, order, a in pieces])
    output = None
    for tm_masks in ((0,), tuple(1 << b for b in range(tm_bits)), None):
        pieces = []
        for per_slab in zip(*found):
            mask, order = per_slab[0][:2]
            late = mask != 0 and mask & (mask - 1) != 0
            if late if tm_masks is None else mask in tm_masks:
                pieces.append(([(mask, o) for o in order], [f[2] for f in per_slab]))
                pieces.append(([(mask, o ^ 1) for o in order], [f[3] for f in per_slab]))
        if pieces:
            output = contract(kernel, pieces, output, devices, rows, space_bits)
    return output[None]


def solution(mesh):
    in_specs = (
        P("tm", None, None, "space", None),
        P(("tm", "space"), None, None, None),
        P(("tm", "space"), None),
        P(("tm", "space"), None),
        P(),
    )
    out_specs = P(("tm", "space"), None, None, None, None)
    return jax.shard_map(body, mesh=mesh, in_specs=in_specs, out_specs=out_specs, check_vma=False)
```
